32 devices in a mesh: groups: 2 (over x), win: 16 (over z, y, core).
Axes of the slice: x: 2, y: 2, z: 4, core: 2. Of those that a mesh axis runs over, the one named last changes fastest.
Arguments:
- latents: bfloat16 [6, 8, 256, 1536], P('groups', None, 'win'), parts along dimension 0, may hold values from -60 to 60
- offsets: int32 [6], P('groups'), parts along dimension 0, may hold values from 0 to 8, as said below
- levels: int32 [6], P('groups'), parts along dimension 0, may hold values from 0 to 31
- mod_table: bfloat16 [32, 6, 1536], replicated, may hold values from -3 to 3
- rel_bias: float32 [6, 64, 64], replicated, may hold values from -3 to 403
- w_qkv: bfloat16 [1536, 2304], P('win'), may hold values from -0.15625 to 0.15625
- w_out: bfloat16 [768, 1536], P('win'), may hold values from -0.21875 to 0.21875
- w_up: bfloat16 [1536, 3072], P('win'), may hold values from -0.15625 to 0.15625
- w_down: bfloat16 [3072, 1536], P('win'), may hold values from -0.109375 to 0.109375
Outputs:
- result: bfloat16 [6, 8, 256, 1536], P('groups', None, 'win'), parts along dimension 0
The draws below stay inside these ranges and needn't reach their ends.
There are 2 independent parts, one for each index of `groups`. The reference program is written for one: setup_inputs(seed, part) draws one part's arguments, and reference() takes and returns one part's arrays. A program takes and returns all parts, laid end to end along the dimension named above; an argument that names none is the same for every part. Nothing has to cross between parts.
Inputs may be any that keep to these rules, and one draw needn't show every extreme that they name: `offsets`: some micro-batch has offset 8 in every draw.
All inputs are finite; a program needn't handle non-finite values.
Results may differ from the reference program's by a relative error of at most 0.007.
Values may be sent and summed in bfloat16 or wider, within the bound.
A program may use at most 128 MiB of HBM per device.

```python
import jax
import jax.numpy as jnp
from jax import lax

D = 1536
HEADS = 6
HEAD_DIM = 128
FF = 3072
WIN = 8
LEVELS = 32
MB = 3
LON = 256


def draw_latents(key, part):
    first = jax.random.fold_in(jax.random.fold_in(key, 11), 0)
    base = jax.random.normal(first, (MB, WIN, LON, D), jnp.float32)
    return jnp.clip(base, -6.0, 6.0).astype(jnp.bfloat16)


def draw_rel_bias(key, part):
    keys = jax.random.split(jax.random.fold_in(key, 23), 1)
    width = WIN * WIN
    base = jnp.clip(jax.random.normal(keys[0], (HEADS, width, width), jnp.float32), -3.0, 3.0)
    return base.astype(jnp.float32)


def draw_offsets(key, part):
    first, second = jax.random.split(jax.random.fold_in(key, 37))
    values_drawn = jax.random.randint(first, (MB,), 0, WIN + 1)
    place = jax.random.randint(second, (), 0, MB)
    return jnp.where(jnp.arange(MB, dtype=jnp.int32) == place, WIN, values_drawn).astype(jnp.int32)


def block_levels(key, dims, shards, least, top_value):
    def one(dim, blocks):
        draws = jax.random.uniform(jax.random.fold_in(jax.random.fold_in(key, 6), dim), (blocks,), jnp.float32, least / len(shards), top_value / len(shards))
        return jnp.repeat(jnp.exp(draws), dims[dim] // blocks).reshape((-1,) + (1,) * (len(dims) - dim - 1))

    level = one(*shards[0])
    for cut in shards[1:]:
        level = level * one(*cut)
    return level


def bell_draw(key, extent, scale, most, shards=(), kind=jnp.bfloat16):
    factor_of = block_levels(key, extent, shards, -0.22, 0.18) if shards else 1.0
    drawn = jax.random.normal(key, extent, jnp.float32) * scale * factor_of
    return jnp.minimum(jnp.maximum(drawn, -most), most).astype(kind)


def setup_inputs(seed: int = 0, part: int = 0) -> dict:
    splits = jax.random.split(jax.random.key(seed), 10)
    part_splits = jax.random.split(jax.random.fold_in(splits[9], part), 10)
    return {
        "latents": draw_latents(jax.random.fold_in(jax.random.fold_in(splits[9], part), 71), part),
        "offsets": draw_offsets(jax.random.fold_in(jax.random.fold_in(splits[9], part), 71), part),
        "levels": jax.random.randint(part_splits[2], (MB,), 0, LEVELS).astype(jnp.int32),
        "mod_table": bell_draw(splits[3], (LEVELS, 6, D), 0.5, 3.0),
        "rel_bias": draw_rel_bias(jax.random.fold_in(splits[9], 71), part),
        "w_qkv": bell_draw(splits[5], (D, 3 * HEADS * HEAD_DIM), D ** -0.5, 0.15625, ((0, 16),)),
        "w_out": bell_draw(splits[6], (HEADS * HEAD_DIM, D), (HEADS * HEAD_DIM) ** -0.5, 0.21875, ((0, 16),)),
        "w_up": bell_draw(splits[7], (D, FF), D ** -0.5, 0.15625, ((0, 16),)),
        "w_down": bell_draw(splits[8], (FF, D), FF ** -0.5, 0.109375, ((0, 16),)),
    }


def norm_rows(values_in):
    centre = values_in - lax.optimization_barrier(jnp.mean(values_in, axis=-1, keepdims=True))
    spread = lax.optimization_barrier(jnp.mean(centre * centre, axis=-1, keepdims=True))
    return centre * lax.rsqrt(spread + 1e-06)

def reference(latents, offsets, levels, mod_table, rel_bias, w_qkv, w_out, w_up, w_down):
    batches, lat_rows, columns, features = latents.shape
    inner = HEADS * HEAD_DIM
    selector = (levels[:, None] == jnp.arange(LEVELS, dtype=jnp.int32)[None, :]).astype(jnp.float32)
    modulation = jnp.einsum('ml,lkd->mkd', selector, mod_table.astype(jnp.float32))
    modulation = modulation.reshape(batches, 6, 1, 1, features)
    stream = latents.astype(jnp.float32)
    normed = (norm_rows(stream) * (1.0 + modulation[:, 0]) + modulation[:, 1]).astype(jnp.bfloat16)
    rolled = jax.vmap(lambda region, shift_by: jnp.roll(region, shift_by, axis=1))(normed, offsets)
    per_row = columns // WIN
    windows = rolled.reshape(batches, lat_rows, per_row, WIN, features).transpose(0, 2, 1, 3, 4)
    windows = windows.reshape(-1, lat_rows * WIN, features)
    number = windows.shape[0]
    triple = jnp.dot(windows.reshape(-1, features), w_qkv, preferred_element_type=jnp.float32)
    triple = triple.astype(jnp.bfloat16).reshape(number, lat_rows * WIN, 3, HEADS, HEAD_DIM)
    triple = triple.astype(jnp.float32)
    scores = jnp.einsum('wqhe,wkhe->whqk', triple[:, :, 0], triple[:, :, 1]) * (1.0 / HEAD_DIM ** 0.5)
    scores = scores + rel_bias[None]
    probs = jax.nn.softmax(scores, axis=-1).astype(jnp.bfloat16)
    attended = jnp.einsum('whqk,wkhe->wqhe', probs.astype(jnp.float32), triple[:, :, 2]).astype(jnp.bfloat16)
    projected = jnp.dot(attended.reshape(-1, inner), w_out, preferred_element_type=jnp.float32)
    projected = projected.reshape(batches, per_row, lat_rows, WIN, features).transpose(0, 2, 1, 3, 4)
    projected = projected.reshape(batches, lat_rows, columns, features)
    projected = jax.vmap(lambda region, shift_by: jnp.roll(region, -shift_by, axis=1))(projected, offsets)
    middle = (stream + modulation[:, 2] * projected).astype(jnp.bfloat16)
    second = (norm_rows(middle.astype(jnp.float32)) * (1.0 + modulation[:, 3]) + modulation[:, 4]).astype(jnp.bfloat16)
    hidden = jnp.dot(second.reshape(-1, features), w_up, preferred_element_type=jnp.float32)
    hidden = jax.nn.gelu(hidden, approximate=False).astype(jnp.bfloat16)
    lowered = jnp.dot(hidden, w_down, preferred_element_type=jnp.float32).reshape(batches, lat_rows, columns, features)
    return (middle.astype(jnp.float32) + modulation[:, 5] * lowered).astype(jnp.bfloat16)
```

```python
import functools

import jax
import jax.numpy as jnp
from jax import lax
from jax.experimental import pallas as pl
from jax.experimental.pallas import tpu as pltpu
from jax.sharding import PartitionSpec as P

HEADS = 6
HEAD_DIM = 128
WIN = 8
LEVELS = 32

MESH = pl.DeviceIdType.MESH
SLOTS = 25


class Gather:
    def __init__(self, ring, shards, fulls, send, recv, local):
        self.ring, self.shards, self.fulls = ring, shards, fulls
        self.send, self.recv, self.local = send, recv, local
        me = lax.axis_index("win")
        self.c = lax.rem(me, 2)
        self.y = lax.rem(me // 2, 2)
        self.z = me // 4
        self.g = lax.axis_index("groups")
        self.h = lax.rem(self.g, 2)
        up, down = lax.rem(self.z + 1, ring), lax.rem(self.z + ring - 1, ring)
        self.across = lax.rem(self.z + 2, ring)
        self.up, self.down = up, down
        self.to_up = {"win": self.place(up, self.y, self.c)}
        self.to_down = {"win": self.place(down, self.y, self.c)}
        self.to_y = {"win": self.place(self.z, 1 - self.y, self.c)}
        self.to_core = {"win": self.place(self.z, self.y, 1 - self.c)}
        self.to_x = {"groups": self.g + 1 - 2 * self.h}
        self.started = []

    def place(self, z, y, c):
        return (z * 2 + y) * 2 + c

    def neighbours(self):
        return [self.to_up, self.to_down, self.to_y, self.to_core, self.to_x]

    def half(self, t, h):
        width = self.shards[t].shape[1] // 2
        return pl.ds(pl.multiple_of(h * width, 128), width)

    def part(self, t, z, y, c, h=None):
        depth = self.shards[t].shape[0]
        rows = pl.ds(pl.multiple_of(self.place(z, y, c) * depth, depth), depth)
        return self.fulls[t].at[rows] if h is None else self.fulls[t].at[rows, self.half(t, h)]

    def copy(self, t, slot, src, dst, to):
        at = t * SLOTS + slot
        return pltpu.make_async_remote_copy(
            src_ref=src,
            dst_ref=dst,
            send_sem=self.send.at[at],
            recv_sem=self.recv.at[at],
            device_id=to,
            device_id_type=MESH,
        )

    def put(self, t, slot, src, dst, to):
        made = self.copy(t, slot, src, dst, to)
        made.start()
        self.started.append(made)

    def pass_on(self, t, slot, part, to):
        self.put(t, slot, part, part, to)

    def arrive(self, t, slot, part):
        self.copy(t, slot, part, part, self.to_core).wait_recv()

    def own(self, t):
        shard = self.shards[t]
        mine = self.part(t, self.z, self.y, self.c)
        half = self.part(t, self.z, self.y, self.c, self.h)
        self.put(t, 0, shard, mine, self.to_up)
        self.put(t, 1, shard, mine, self.to_down)
        self.put(t, 4, shard.at[:, self.half(t, self.h)], half, self.to_y)
        self.put(t, 12, shard, mine, self.to_core)
        pltpu.make_async_copy(shard, mine, self.local.at[t]).start()

    def near(self, t):
        for slot, z, half, to in ((0, self.down, 0, self.to_up), (1, self.up, 1, self.to_down)):
            whole = self.part(t, z, self.y, self.c)
            self.arrive(t, slot, whole)
            self.pass_on(t, 2 + slot, self.part(t, z, self.y, self.c, half), to)
            self.pass_on(t, 5 + slot, self.part(t, z, self.y, self.c, self.h), self.to_y)
            self.pass_on(t, 13 + slot, whole, self.to_core)

    def far(self, t):
        for half in (0, 1):
            part = self.part(t, self.across, self.y, self.c, half)
            self.arrive(t, 2 + half, part)
            self.pass_on(t, 15 + half, part, self.to_core)
        self.pass_on(t, 7, self.part(t, self.across, self.y, self.c, self.h), self.to_y)

    def turn(self, t, k):
        z = (self.z, self.down, self.up, self.across)[k]
        part = self.part(t, z, 1 - self.y, self.c, self.h)
        self.arrive(t, 4 + k, part)
        self.pass_on(t, 8 + k, part, self.to_x)
        self.pass_on(t, 17 + k, part, self.to_core)

    def last(self, t, k):
        z = (self.z, self.down, self.up, self.across)[k]
        part = self.part(t, z, 1 - self.y, self.c, 1 - self.h)
        self.arrive(t, 8 + k, part)
        self.pass_on(t, 21 + k, part, self.to_core)

    def handed(self, t):
        other = 1 - self.c
        zs = (self.z, self.down, self.up, self.across)
        mine = self.part(t, self.z, self.y, self.c)
        pltpu.make_async_copy(self.shards[t], mine, self.local.at[t]).wait()
        for k in range(3):
            self.arrive(t, 12 + k, self.part(t, zs[k], self.y, other))
        for half in (0, 1):
            self.arrive(t, 15 + half, self.part(t, self.across, self.y, other, half))
        for k in range(4):
            self.arrive(t, 17 + k, self.part(t, zs[k], 1 - self.y, other, self.h))
        for k in range(4):
            self.arrive(t, 21 + k, self.part(t, zs[k], 1 - self.y, other, 1 - self.h))

    def drain(self):
        for made in self.started:
            made.wait_send()


def meet(neighbours):
    barrier = pltpu.get_barrier_semaphore()
    for to in neighbours:
        pl.semaphore_signal(barrier, inc=1, device_id=to, device_id_type=MESH)
    pl.semaphore_wait(barrier, len(neighbours))


def gather_kernel(ring, *refs):
    shards, fulls = refs[:4], refs[4:8]
    gather = Gather(ring, shards, fulls, *refs[8:])
    meet(gather.neighbours())
    gather.own(0)
    gather.own(1)
    for t in range(4):
        gather.near(t)
        gather.turn(t, 0)
        gather.far(t)
        if t + 2 < 4:
            gather.own(t + 2)
        for k in (1, 2, 3):
            gather.turn(t, k)
        for k in range(4):
            gather.last(t, k)
    for t in range(4):
        gather.handed(t)
    gather.drain()


def gather_all(shards):
    count = lax.axis_size("win")
    if count // 4 != 4 or lax.axis_size("groups") % 2:
        return [lax.all_gather(shard, "win", axis=0, tiled=True) for shard in shards]
    full = [jax.ShapeDtypeStruct((s.shape[0] * count, s.shape[1]), s.dtype) for s in shards]
    return pl.pallas_call(
        functools.partial(gather_kernel, count // 4),
        out_shape=full,
        in_specs=[pl.BlockSpec(memory_space=pltpu.VMEM)] * 4,
        out_specs=[pl.BlockSpec(memory_space=pl.ANY)] * 4,
        scratch_shapes=[
            pltpu.SemaphoreType.DMA((4 * SLOTS,)),
            pltpu.SemaphoreType.DMA((4 * SLOTS,)),
            pltpu.SemaphoreType.DMA((4,)),
        ],
        compiler_params=pltpu.CompilerParams(collective_id=0, has_side_effects=True),
    )(*shards)


def passed_along(shard, axis, by):
    length = lax.axis_size(axis)
    return lax.ppermute(shard, axis, [(i, (i + by) % length) for i in range(length)])


def norm_rows(values_in):
    centre = values_in - jnp.mean(values_in, axis=-1, keepdims=True)
    spread = jnp.mean(centre * centre, axis=-1, keepdims=True)
    return centre * lax.rsqrt(spread + 1e-06)


def restore_grid(region, arrived, offsets, columns):
    widened = jnp.concatenate([region, arrived], axis=2)
    return jax.vmap(lambda plane, shift_by: lax.dynamic_slice_in_dim(plane, shift_by, columns, 1))(
        widened, offsets
    )


def local(latents, offsets, levels, mod_table, rel_bias, w_qkv, w_out, w_up, w_down):
    batches, lat_rows, columns, features = latents.shape
    full_qkv, full_out, full_up, full_down = gather_all((w_qkv, w_out, w_up, w_down))
    inner = HEADS * HEAD_DIM
    per_dev = columns // WIN
    selector = (levels[:, None] == jnp.arange(LEVELS, dtype=jnp.int32)[None, :]).astype(
        jnp.bfloat16
    )
    modulation = jnp.dot(
        selector, mod_table.reshape(LEVELS, 6 * features), preferred_element_type=jnp.float32
    )
    modulation = modulation.reshape(batches, 6, 1, 1, features)
    stream = latents.astype(jnp.float32)
    normed = (norm_rows(stream) * (1.0 + modulation[:, 0]) + modulation[:, 1]).astype(jnp.bfloat16)
    arrived = passed_along(normed[:, :, columns - WIN :, :], "win", 1)
    widened = jnp.concatenate([arrived, normed], axis=2)
    rolled = jax.vmap(
        lambda plane, shift_by: lax.dynamic_slice_in_dim(plane, WIN - shift_by, columns, 1)
    )(widened, offsets)
    windows = rolled.reshape(batches, lat_rows, per_dev, WIN, features).transpose(0, 2, 1, 3, 4)
    windows = windows.reshape(-1, lat_rows * WIN, features)
    number = windows.shape[0]
    triple = jnp.dot(windows.reshape(-1, features), full_qkv, preferred_element_type=jnp.float32)
    triple = triple.astype(jnp.bfloat16).reshape(number, lat_rows * WIN, 3, HEADS, HEAD_DIM)
    scores = jnp.einsum(
        "wqhe,wkhe->whqk", triple[:, :, 0], triple[:, :, 1], preferred_element_type=jnp.float32
    )
    scores = scores * (1.0 / HEAD_DIM**0.5) + rel_bias[None]
    probs = jax.nn.softmax(scores, axis=-1).astype(jnp.bfloat16)
    attended = jnp.einsum(
        "whqk,wkhe->wqhe", probs, triple[:, :, 2], preferred_element_type=jnp.float32
    ).astype(jnp.bfloat16)
    attended = attended.reshape(batches, per_dev, lat_rows, WIN, inner).transpose(0, 2, 1, 3, 4)
    attended = attended.reshape(batches, lat_rows, columns, inner)
    returned = passed_along(attended[:, :, :WIN, :], "win", -1)
    restored = restore_grid(attended, returned, offsets, columns)
    projected = jnp.dot(restored.reshape(-1, inner), full_out, preferred_element_type=jnp.float32)
    projected = projected.reshape(batches, lat_rows, columns, features)
    middle = (stream + modulation[:, 2] * projected).astype(jnp.bfloat16)
    second = (
        norm_rows(middle.astype(jnp.float32)) * (1.0 + modulation[:, 3]) + modulation[:, 4]
    ).astype(jnp.bfloat16)
    hidden = jnp.dot(second.reshape(-1, features), full_up, preferred_element_type=jnp.float32)
    hidden = jax.nn.gelu(hidden, approximate=False).astype(jnp.bfloat16)
    lowered = jnp.dot(hidden, full_down, preferred_element_type=jnp.float32).reshape(
        batches, lat_rows, columns, features
    )
    return (middle.astype(jnp.float32) + modulation[:, 5] * lowered).astype(jnp.bfloat16)


def solution(mesh):
    in_specs = (
        P("groups", None, "win", None),
        P("groups"),
        P("groups"),
        P(),
        P(),
        P("win", None),
        P("win", None),
        P("win", None),
        P("win", None),
    )
    out_specs = P("groups", None, "win", None)
    return jax.shard_map(local, mesh=mesh, in_specs=in_specs, out_specs=out_specs, check_vma=False)
```

```python
import functools

import jax
import jax.numpy as jnp
from jax import lax
from jax.experimental import pallas as pl
from jax.experimental.pallas import tpu as pltpu
from jax.sharding import PartitionSpec as P

HEADS = 6
HEAD_DIM = 128
WIN = 8
LEVELS = 32

MESH = pl.DeviceIdType.MESH
SLOTS = 28
LINE = 4
UP, DOWN, ALONG_Y, ALONG_X, FAR_X, HAND, HAND_FAR, HAND_Y, HAND_X = 0, 3, 6, 10, 14, 15, 19, 20, 24

ORDER = (
    (1, 1), (0, 2), (1, 2), (0, 3), (3, 0), (2, 1), (1, 3), (0, 4), (0, 5), (1, 4), (1, 5), (2, 2),
    (2, 3), (3, 1), (2, 4), (3, 2), (2, 5), (3, 3), (3, 4), (3, 5),
)


def under(condition, act):
    if condition is None:
        act()
    else:
        pl.when(condition)(act)


class Gather:
    def __init__(self, shards, fulls, send, recv, local):
        self.shards, self.fulls = shards, fulls
        self.send, self.recv, self.local = send, recv, local
        me = lax.axis_index("win")
        self.c = lax.rem(me, 2)
        self.y = lax.rem(me // 2, 2)
        self.z = me // 4
        self.g = lax.axis_index("groups")
        self.h = lax.rem(self.g, 2)
        up, down = lax.rem(self.z + 1, LINE), lax.rem(self.z + LINE - 1, LINE)
        self.to_up = {"win": self.place(up, self.y, self.c)}
        self.to_down = {"win": self.place(down, self.y, self.c)}
        self.to_y = {"win": self.place(self.z, 1 - self.y, self.c)}
        self.to_core = {"win": self.place(self.z, self.y, 1 - self.c)}
        self.to_x = {"groups": self.g + 1 - 2 * self.h}
        self.started = []

    def place(self, z, y, c):
        return (z * 2 + y) * 2 + c

    def neighbours(self):
        return [self.to_up, self.to_down, self.to_y, self.to_core, self.to_x]

    def half(self, t, h):
        width = self.shards[t].shape[1] // 2
        return pl.ds(pl.multiple_of(h * width, 128), width)

    def part(self, t, z, y, c, h=None):
        depth = self.shards[t].shape[0]
        rows = pl.ds(pl.multiple_of(self.place(z, y, c) * depth, depth), depth)
        return self.fulls[t].at[rows] if h is None else self.fulls[t].at[rows, self.half(t, h)]

    def copy(self, t, slot, src, dst, to):
        at = t * SLOTS + slot
        return pltpu.make_async_remote_copy(
            src_ref=src,
            dst_ref=dst,
            send_sem=self.send.at[at],
            recv_sem=self.recv.at[at],
            device_id=to,
            device_id_type=MESH,
        )

    def put(self, condition, make):
        under(condition, lambda: make().start())
        self.started.append((condition, make))

    def pass_on(self, condition, t, slot, part, to):
        self.put(condition, lambda: self.copy(t, slot, part(), part(), to))

    def arrive(self, condition, t, slot, part):
        under(condition, lambda: self.copy(t, slot, part(), part(), self.to_core).wait_recv())

    def mine(self, t, z, h=None):
        return lambda: self.part(t, z, self.y, self.c, h)

    def own(self, t):
        shard = self.shards[t]
        mine, half = self.mine(t, self.z), self.mine(t, self.z, self.h)
        up, down = self.z + 1 < LINE, self.z >= 1
        self.put(up, lambda: self.copy(t, UP, shard, mine(), self.to_up))
        self.put(down, lambda: self.copy(t, DOWN, shard, mine(), self.to_down))
        source = shard.at[:, self.half(t, self.h)]
        self.put(None, lambda: self.copy(t, ALONG_Y + self.z, source, half(), self.to_y))
        self.put(None, lambda: self.copy(t, HAND + self.z, shard, mine(), self.to_core))
        pltpu.make_async_copy(shard, mine(), self.local.at[t]).start()

    def sources(self, d):
        return ((self.z >= d, self.z - d), (self.z + d < LINE, self.z + d))

    def come(self, t, d):
        ways = ((UP, self.z + 1 < LINE, self.to_up), (DOWN, self.z >= 1, self.to_down))
        h = self.h if d == 3 else None
        for (there, z), (way, more, to) in zip(self.sources(d), ways):
            part = self.mine(t, z, h)
            self.arrive(there, t, way + d - 1, part)
            if d < 3:
                onward = self.mine(t, z, self.h if d == 2 else None)
                self.pass_on(there & more, t, way + d, onward, to)
            self.pass_on(there, t, ALONG_Y + z, self.mine(t, z, self.h), self.to_y)
            if d == 3:
                self.pass_on(there, t, FAR_X, part, self.to_x)
            self.pass_on(there, t, HAND + z, part, self.to_core)

    def at(self, d):
        return ((None, self.z),) if d == 0 else self.sources(d)

    def turn(self, t, d):
        for there, z in self.at(d):
            part = lambda z=z: self.part(t, z, 1 - self.y, self.c, self.h)
            self.arrive(there, t, ALONG_Y + z, part)
            self.pass_on(there, t, ALONG_X + z, part, self.to_x)
            self.pass_on(there, t, HAND_Y + z, part, self.to_core)

    def last(self, t, d):
        for there, z in self.at(d):
            part = lambda z=z: self.part(t, z, 1 - self.y, self.c, 1 - self.h)
            self.arrive(there, t, ALONG_X + z, part)
            self.pass_on(there, t, HAND_X + z, part, self.to_core)

    def other(self, t):
        for there, z in self.sources(3):
            part = self.mine(t, z, 1 - self.h)
            self.arrive(there, t, FAR_X, part)
            self.pass_on(there, t, HAND_FAR, part, self.to_core)

    def handed(self, t):
        core = 1 - self.c
        pltpu.make_async_copy(self.shards[t], self.mine(t, self.z)(), self.local.at[t]).wait()
        for d in range(LINE):
            for there, z in self.at(d):
                for slot, y, h in (
                    (HAND + z, self.y, self.h if d == 3 else None),
                    (HAND_Y + z, 1 - self.y, self.h),
                    (HAND_X + z, 1 - self.y, 1 - self.h),
                ):
                    part = lambda z=z, y=y, h=h: self.part(t, z, y, core, h)
                    self.arrive(there, t, slot, part)
        for there, z in self.sources(3):
            part = lambda z=z: self.part(t, z, self.y, core, 1 - self.h)
            self.arrive(there, t, HAND_FAR, part)

    def stage(self, t, number):
        if number == 0:
            return [lambda: self.own(t)]
        events = []
        if number <= 3:
            events.append(lambda: self.come(t, number))
        if number == 4:
            events.append(lambda: self.other(t))
        if 1 <= number <= 4:
            events.append(lambda: self.turn(t, number - 1))
        if 2 <= number <= 5:
            events.append(lambda: self.last(t, number - 2))
        if number == 5:
            events.append(lambda: self.handed(t))
        return events

    def drain(self):
        for condition, make in self.started:
            under(condition, lambda make=make: make().wait_send())


def meet(neighbours):
    barrier = pltpu.get_barrier_semaphore()
    for to in neighbours:
        pl.semaphore_signal(barrier, inc=1, device_id=to, device_id_type=MESH)
    pl.semaphore_wait(barrier, len(neighbours))


def passed_along(shard, axis, by):
    length = lax.axis_size(axis)
    return lax.ppermute(shard, axis, [(i, (i + by) % length) for i in range(length)])


def norm_rows(values_in):
    centre = values_in - jnp.mean(values_in, axis=-1, keepdims=True)
    spread = jnp.mean(centre * centre, axis=-1, keepdims=True)
    return centre * lax.rsqrt(spread + 1e-06)


def restore_grid(region, arrived, offsets, columns):
    widened = jnp.concatenate([region, arrived], axis=2)
    return jax.vmap(lambda plane, shift_by: lax.dynamic_slice_in_dim(plane, shift_by, columns, 1))(
        widened, offsets
    )


def plain(latents, offsets, levels, mod_table, rel_bias, w_qkv, w_out, w_up, w_down):
    batches, lat_rows, columns, features = latents.shape
    inner = HEADS * HEAD_DIM
    per_dev = columns // WIN
    selector = (levels[:, None] == jnp.arange(LEVELS, dtype=jnp.int32)[None, :]).astype(
        jnp.bfloat16
    )
    modulation = jnp.dot(
        selector, mod_table.reshape(LEVELS, 6 * features), preferred_element_type=jnp.float32
    )
    modulation = modulation.reshape(batches, 6, 1, 1, features)
    stream = latents.astype(jnp.float32)
    normed = (norm_rows(stream) * (1.0 + modulation[:, 0]) + modulation[:, 1]).astype(jnp.bfloat16)
    arrived = passed_along(normed[:, :, columns - WIN :, :], "win", 1)
    widened = jnp.concatenate([arrived, normed], axis=2)
    rolled = jax.vmap(
        lambda plane, shift_by: lax.dynamic_slice_in_dim(plane, WIN - shift_by, columns, 1)
    )(widened, offsets)
    full_qkv = lax.all_gather(w_qkv, "win", axis=0, tiled=True)
    windows = rolled.reshape(batches, lat_rows, per_dev, WIN, features).transpose(0, 2, 1, 3, 4)
    windows = windows.reshape(-1, lat_rows * WIN, features)
    number = windows.shape[0]
    triple = jnp.dot(windows.reshape(-1, features), full_qkv, preferred_element_type=jnp.float32)
    triple = triple.astype(jnp.bfloat16).reshape(number, lat_rows * WIN, 3, HEADS, HEAD_DIM)
    scores = jnp.einsum(
        "wqhe,wkhe->whqk", triple[:, :, 0], triple[:, :, 1], preferred_element_type=jnp.float32
    )
    scores = scores * (1.0 / HEAD_DIM**0.5) + rel_bias[None]
    probs = jax.nn.softmax(scores, axis=-1).astype(jnp.bfloat16)
    attended = jnp.einsum(
        "whqk,wkhe->wqhe", probs, triple[:, :, 2], preferred_element_type=jnp.float32
    ).astype(jnp.bfloat16)
    attended = attended.reshape(batches, per_dev, lat_rows, WIN, inner).transpose(0, 2, 1, 3, 4)
    attended = attended.reshape(batches, lat_rows, columns, inner)
    full_out = lax.all_gather(w_out, "win", axis=0, tiled=True)
    returned = passed_along(attended[:, :, :WIN, :], "win", -1)
    restored = restore_grid(attended, returned, offsets, columns)
    projected = jnp.dot(restored.reshape(-1, inner), full_out, preferred_element_type=jnp.float32)
    projected = projected.reshape(batches, lat_rows, columns, features)
    middle = (stream + modulation[:, 2] * projected).astype(jnp.bfloat16)
    second = (
        norm_rows(middle.astype(jnp.float32)) * (1.0 + modulation[:, 3]) + modulation[:, 4]
    ).astype(jnp.bfloat16)
    full_up = lax.all_gather(w_up, "win", axis=0, tiled=True)
    hidden = jnp.dot(second.reshape(-1, features), full_up, preferred_element_type=jnp.float32)
    hidden = jax.nn.gelu(hidden, approximate=False).astype(jnp.bfloat16)
    full_down = lax.all_gather(w_down, "win", axis=0, tiled=True)
    lowered = jnp.dot(hidden, full_down, preferred_element_type=jnp.float32).reshape(
        batches, lat_rows, columns, features
    )
    return (middle.astype(jnp.float32) + modulation[:, 5] * lowered).astype(jnp.bfloat16)


def spread(work, events):
    done = 0
    for index, piece in enumerate(work):
        piece()
        upto = (len(events) * (index + 1)) // len(work)
        for event in events[done:upto]:
            event()
        done = upto


def pieces(count, step, act):
    def piece(first):
        lax.fori_loop(first, min(first + step, count), lambda i, _: (act(i), 0)[1], 0)

    return [functools.partial(piece, first) for first in range(0, count, step)]


def kernel(
    batches, block, area, lat_ref, low_ref, high_ref, mod_ref, gather_in_ref, gather_out_ref,
    bias_ref, s0, s1, s2, s3, out_ref, f0, f1, f2, f3, prev, after, normed, wins, triple, heads,
    restored, middle, second, hidden, send, recv, local, halo_send, halo_recv,
):
    features = lat_ref.shape[1]
    inner = HEADS * HEAD_DIM
    own = lat_ref.shape[0] // batches
    side = low_ref.shape[0] // batches
    wide = own + 2 * side
    moved = wins.shape[0] // batches
    gather = Gather((s0, s1, s2, s3), (f0, f1, f2, f3), send, recv, local)
    me, count = lax.axis_index("win"), lax.axis_size("win")
    right, left = {"win": lax.rem(me + 1, count)}, {"win": lax.rem(me + count - 1, count)}
    meet(gather.neighbours() + [right, left])
    halos = []
    for at, src, dst, to in ((0, high_ref, prev, right), (1, low_ref, after, left)):
        made = pltpu.make_async_remote_copy(
            src_ref=src,
            dst_ref=dst,
            send_sem=halo_send.at[at],
            recv_sem=halo_recv.at[at],
            device_id=to,
            device_id_type=MESH,
        )
        made.start()
        halos.append(made)
    gather.own(0)
    gather.own(1)

    def norm_into(src, first, dst, start, m, scale, shift):
        rows = src[pl.ds(first, block), :].astype(jnp.float32)
        value = norm_rows(rows) * (1.0 + mod_ref[m, pl.ds(scale, 1), :])
        value = value + mod_ref[m, pl.ds(shift, 1), :]
        dst[pl.ds(start, block), :] = value.astype(jnp.bfloat16)

    for m in range(batches):
        def norm_own(i, _):
            norm_into(lat_ref, m * own + i * block, normed, m * wide + side + i * block, m, 0, 1)
            return 0

        lax.fori_loop(0, own // block, norm_own, 0)
    gather.come(0, 1)
    for made in halos:
        made.wait()
    for m in range(batches):
        for src, base in ((prev, 0), (after, side + own)):
            def norm_side(i, _):
                norm_into(src, m * side + i * block, normed, m * wide + base + i * block, m, 0, 1)
                return 0

            lax.fori_loop(0, side // block, norm_side, 0)
    gather.turn(0, 0)
    gather.own(2)

    def arrange(m):
        rows = normed[pl.ds(pl.multiple_of(m * wide, 16), wide), :]
        wins[pl.ds(pl.multiple_of(m * moved, 16), moved), :] = jnp.dot(
            gather_in_ref[m], rows, preferred_element_type=jnp.float32
        ).astype(jnp.bfloat16)

    width = 256

    def columns(i):
        return pl.ds(pl.multiple_of(i * width, width), width)

    def project(i):
        triple[:, columns(i)] = jnp.dot(
            wins[...], f0[:, columns(i)], preferred_element_type=jnp.float32
        ).astype(jnp.bfloat16)

    def attend(w):
        rows = pl.ds(pl.multiple_of(w * area, area), area)
        for head in range(HEADS):
            def of(which):
                return triple[rows, pl.ds(which * inner + head * HEAD_DIM, HEAD_DIM)]

            scores = lax.dot_general(
                of(0), of(1), (((1,), (1,)), ((), ())), preferred_element_type=jnp.float32
            )
            scores = scores * (1.0 / HEAD_DIM**0.5) + bias_ref[head]
            powers = jnp.exp(scores - jnp.max(scores, axis=-1, keepdims=True))
            probs = (powers / jnp.sum(powers, axis=-1, keepdims=True)).astype(jnp.bfloat16)
            heads[rows, pl.ds(head * HEAD_DIM, HEAD_DIM)] = jnp.dot(
                probs, of(2), preferred_element_type=jnp.float32
            ).astype(jnp.bfloat16)

    def restore(m):
        rows = heads[pl.ds(pl.multiple_of(m * moved, 16), moved), :]
        restored[pl.ds(pl.multiple_of(m * own, 16), own), :] = jnp.dot(
            gather_out_ref[m], rows, preferred_element_type=jnp.float32
        ).astype(jnp.bfloat16)

    def add(base_ref, dst, found, which, i):
        for m in range(batches):
            rows = pl.ds(m * own, own)
            change = mod_ref[m, pl.ds(which, 1), columns(i)] * found[m * own : (m + 1) * own]
            dst[rows, columns(i)] = (
                base_ref[rows, columns(i)].astype(jnp.float32) + change
            ).astype(jnp.bfloat16)

    def settle(i):
        found = jnp.dot(restored[...], f1[:, columns(i)], preferred_element_type=jnp.float32)
        add(lat_ref, middle, found, 2, i)

    def lift(i):
        found = jnp.dot(second[...], f2[:, columns(i)], preferred_element_type=jnp.float32)
        found = 0.5 * found * (1.0 + lax.erf(found * (0.5**0.5)))
        hidden[:, columns(i)] = found.astype(jnp.bfloat16)

    def lower(i):
        found = jnp.dot(hidden[...], f3[:, columns(i)], preferred_element_type=jnp.float32)
        add(middle, out_ref, found, 5, i)

    for m in range(batches):
        arrange(m)
    lined = [(t, event) for t, number in ORDER for event in gather.stage(t, number)]
    index = max(i for i, (t, _) in enumerate(lined) if t == 0) + 1
    for _, event in lined[:index]:
        event()
    lined = lined[index:]
    index = max(i for i, (t, _) in enumerate(lined) if t == 1) + 1
    work = pieces(triple.shape[1] // width, 3, project) + pieces(wins.shape[0] // area, 2, attend)
    spread(work, [event for _, event in lined[:index]])
    lined = lined[index:]
    for m in range(batches):
        restore(m)
    index = max(i for i, (t, _) in enumerate(lined) if t == 2) + 1
    work = pieces(features // width, 3, settle)
    spread(work, [])
    for m in range(batches):
        def norm_again(i, _):
            at = m * own + i * block
            norm_into(middle, at, second, at, m, 3, 4)
            return 0

        lax.fori_loop(0, own // block, norm_again, 0)
    for _, event in lined[:index]:
        event()
    lined = lined[index:]
    spread(pieces(hidden.shape[1] // width, 2, lift), [event for _, event in lined])
    spread(pieces(features // width, features // width, lower), [])
    gather.drain()


def local(latents, offsets, levels, mod_table, rel_bias, w_qkv, w_out, w_up, w_down):
    count = lax.axis_size("win")
    batches, lat_rows, columns, features = latents.shape
    if count != 4 * LINE or lax.axis_size("groups") % 2 or columns < WIN:
        return plain(
            latents, offsets, levels, mod_table, rel_bias, w_qkv, w_out, w_up, w_down
        )
    selector = (levels[:, None] == jnp.arange(LEVELS, dtype=jnp.int32)[None, :]).astype(
        jnp.bfloat16
    )
    modulation = jnp.dot(
        selector, mod_table.reshape(LEVELS, 6 * features), preferred_element_type=jnp.float32
    ).reshape(batches, 6, features)
    area = lat_rows * WIN
    bands = columns // WIN + 1
    own, moved = lat_rows * columns, bands * area
    row = jnp.arange(lat_rows, dtype=jnp.int32)

    def spots(first, size):
        place = first + jnp.arange(size, dtype=jnp.int32)
        both = jnp.broadcast_to(row[:, None], (lat_rows, size)), jnp.broadcast_to(
            place[None], (lat_rows, size)
        )
        return [part.reshape(-1) for part in both]

    def joined(parts):
        return [jnp.concatenate(side) for side in zip(*parts)]

    wide_row, wide_at = joined(
        [spots(0, WIN), spots(WIN, columns), spots(WIN + columns, WIN)]
    )
    rolled_row, rolled_at = joined([spots(band * WIN, WIN) for band in range(bands)])
    own_row, own_at = spots(0, columns)
    by = offsets[:, None, None]
    gather_in = (rolled_row[:, None] == wide_row[None]) & (
        rolled_at[None, :, None] + WIN - by == wide_at[None, None]
    )
    gather_out = (own_row[:, None] == rolled_row[None]) & (
        own_at[None, :, None] + by == rolled_at[None, None]
    )
    low = latents[:, :, :WIN].reshape(-1, features)
    high = latents[:, :, columns - WIN :].reshape(-1, features)
    shards = (w_qkv, w_out, w_up, w_down)
    vmem = pl.BlockSpec(memory_space=pltpu.VMEM)
    total = batches * own
    bf = jnp.bfloat16
    found = pl.pallas_call(
        functools.partial(kernel, batches, 32, area),
        out_shape=jax.ShapeDtypeStruct((total, features), bf),
        in_specs=[vmem] * 11,
        out_specs=vmem,
        scratch_shapes=[pltpu.VMEM((s.shape[0] * count, s.shape[1]), bf) for s in shards]
        + [
            pltpu.VMEM(low.shape, bf),
            pltpu.VMEM(low.shape, bf),
            pltpu.VMEM((batches * (own + 2 * area), features), bf),
            pltpu.VMEM((batches * moved, features), bf),
            pltpu.VMEM((batches * moved, w_qkv.shape[1]), bf),
            pltpu.VMEM((batches * moved, w_out.shape[0] * count), bf),
            pltpu.VMEM((total, w_out.shape[0] * count), bf),
            pltpu.VMEM((total, features), bf),
            pltpu.VMEM((total, features), bf),
            pltpu.VMEM((total, w_up.shape[1]), bf),
            pltpu.SemaphoreType.DMA((4 * SLOTS,)),
            pltpu.SemaphoreType.DMA((4 * SLOTS,)),
            pltpu.SemaphoreType.DMA((4,)),
            pltpu.SemaphoreType.DMA((2,)),
            pltpu.SemaphoreType.DMA((2,)),
        ],
        compiler_params=pltpu.CompilerParams(
            collective_id=0, has_side_effects=True, vmem_limit_bytes=62 * 2**20
        ),
    )(
        latents.reshape(total, features), low, high, modulation, gather_in.astype(bf),
        gather_out.astype(bf), rel_bias, *shards,
    )
    return found.reshape(latents.shape)


def solution(mesh):
    in_specs = (
        P("groups", None, "win", None),
        P("groups"),
        P("groups"),
        P(),
        P(),
        P("win", None),
        P("win", None),
        P("win", None),
        P("win", None),
    )
    out_specs = P("groups", None, "win", None)
    return jax.shard_map(local, mesh=mesh, in_specs=in_specs, out_specs=out_specs, check_vma=False)
```

```python
import functools

import jax
import jax.numpy as jnp
from jax import lax
from jax.experimental import pallas as pl
from jax.experimental.pallas import tpu as pltpu
from jax.sharding import PartitionSpec as P

HEADS = 6
HEAD_DIM = 128
WIN = 8
LEVELS = 32

MESH = pl.DeviceIdType.MESH
SLOTS = 28
LINE = 4
UP, DOWN, ALONG_Y, ALONG_X, FAR_X, HAND, HAND_FAR, HAND_Y, HAND_X = 0, 3, 6, 10, 14, 15, 19, 20, 24

OWN, COME, TURN, LAST, OTHER = range(5)
ORDER = (
    (TURN, 0, 0), (TURN, 1, 0), (COME, 0, 1), (COME, 1, 1), (TURN, 0, 1), (COME, 0, 2),
    (COME, 1, 2), (TURN, 1, 1), (OWN, 2, 0), (LAST, 0, 0), (TURN, 0, 2), (COME, 1, 3),
    (COME, 0, 3), (TURN, 1, 2), (TURN, 1, 3), (LAST, 1, 3), (COME, 2, 1), (TURN, 0, 3),
    (LAST, 1, 0), (TURN, 2, 0), (OTHER, 1, 0), (TURN, 2, 1), (LAST, 1, 2), (OWN, 3, 0),
    (TURN, 3, 0), (OTHER, 0, 0), (LAST, 1, 1), (COME, 2, 2), (LAST, 0, 3), (LAST, 0, 1),
    (LAST, 0, 2), (LAST, 2, 0), (COME, 3, 1), (TURN, 2, 2), (COME, 2, 3), (TURN, 3, 1),
    (COME, 3, 2), (OTHER, 2, 0), (TURN, 2, 3), (LAST, 2, 1), (COME, 3, 3), (LAST, 2, 3),
    (LAST, 2, 2), (TURN, 3, 2), (LAST, 3, 1), (LAST, 3, 0), (TURN, 3, 3), (LAST, 3, 2),
    (OTHER, 3, 0), (LAST, 3, 3),
)


def under(condition, act):
    if condition is None:
        act()
    else:
        pl.when(condition)(act)


class Gather:
    def __init__(self, shards, fulls, send, recv, local):
        self.shards, self.fulls = shards, fulls
        self.send, self.recv, self.local = send, recv, local
        me = lax.axis_index("win")
        self.c = lax.rem(me, 2)
        self.y = lax.rem(me // 2, 2)
        self.z = me // 4
        self.g = lax.axis_index("groups")
        self.h = lax.rem(self.g, 2)
        up, down = lax.rem(self.z + 1, LINE), lax.rem(self.z + LINE - 1, LINE)
        self.to_up = {"win": self.place(up, self.y, self.c)}
        self.to_down = {"win": self.place(down, self.y, self.c)}
        self.to_y = {"win": self.place(self.z, 1 - self.y, self.c)}
        self.to_core = {"win": self.place(self.z, self.y, 1 - self.c)}
        self.to_x = {"groups": self.g + 1 - 2 * self.h}
        self.started = []

    def place(self, z, y, c):
        return (z * 2 + y) * 2 + c

    def neighbours(self):
        return [self.to_up, self.to_down, self.to_y, self.to_core, self.to_x]

    def half(self, t, h):
        width = self.shards[t].shape[1] // 2
        return pl.ds(pl.multiple_of(h * width, 128), width)

    def part(self, t, z, y, c, h=None):
        depth = self.shards[t].shape[0]
        rows = pl.ds(pl.multiple_of(self.place(z, y, c) * depth, depth), depth)
        return self.fulls[t].at[rows] if h is None else self.fulls[t].at[rows, self.half(t, h)]

    def copy(self, t, slot, src, dst, to):
        at = t * SLOTS + slot
        return pltpu.make_async_remote_copy(
            src_ref=src,
            dst_ref=dst,
            send_sem=self.send.at[at],
            recv_sem=self.recv.at[at],
            device_id=to,
            device_id_type=MESH,
        )

    def put(self, condition, make):
        under(condition, lambda: make().start())
        self.started.append((condition, make))

    def pass_on(self, condition, t, slot, part, to):
        self.put(condition, lambda: self.copy(t, slot, part(), part(), to))

    def arrive(self, condition, t, slot, part):
        under(condition, lambda: self.copy(t, slot, part(), part(), self.to_core).wait_recv())

    def mine(self, t, z, h=None):
        return lambda: self.part(t, z, self.y, self.c, h)

    def own(self, t):
        shard = self.shards[t]
        mine, half = self.mine(t, self.z), self.mine(t, self.z, self.h)
        up, down = self.z + 1 < LINE, self.z >= 1
        self.put(up, lambda: self.copy(t, UP, shard, mine(), self.to_up))
        self.put(down, lambda: self.copy(t, DOWN, shard, mine(), self.to_down))
        source = shard.at[:, self.half(t, self.h)]
        self.put(None, lambda: self.copy(t, ALONG_Y + self.z, source, half(), self.to_y))
        self.put(None, lambda: self.copy(t, HAND + self.z, shard, mine(), self.to_core))
        pltpu.make_async_copy(shard, mine(), self.local.at[t]).start()

    def sources(self, d):
        return ((self.z >= d, self.z - d), (self.z + d < LINE, self.z + d))

    def come(self, t, d):
        ways = ((UP, self.z + 1 < LINE, self.to_up), (DOWN, self.z >= 1, self.to_down))
        h = self.h if d == 3 else None
        for (there, z), (way, more, to) in zip(self.sources(d), ways):
            part = self.mine(t, z, h)
            self.arrive(there, t, way + d - 1, part)
            if d < 3:
                onward = self.mine(t, z, self.h if d == 2 else None)
                self.pass_on(there & more, t, way + d, onward, to)
            self.pass_on(there, t, ALONG_Y + z, self.mine(t, z, self.h), self.to_y)
            if d == 3:
                self.pass_on(there, t, FAR_X, part, self.to_x)
            self.pass_on(there, t, HAND + z, part, self.to_core)

    def at(self, d):
        return ((None, self.z),) if d == 0 else self.sources(d)

    def turn(self, t, d):
        for there, z in self.at(d):
            part = lambda z=z: self.part(t, z, 1 - self.y, self.c, self.h)
            self.arrive(there, t, ALONG_Y + z, part)
            self.pass_on(there, t, ALONG_X + z, part, self.to_x)
            self.pass_on(there, t, HAND_Y + z, part, self.to_core)

    def last(self, t, d):
        for there, z in self.at(d):
            part = lambda z=z: self.part(t, z, 1 - self.y, self.c, 1 - self.h)
            self.arrive(there, t, ALONG_X + z, part)
            self.pass_on(there, t, HAND_X + z, part, self.to_core)

    def other(self, t):
        for there, z in self.sources(3):
            part = self.mine(t, z, 1 - self.h)
            self.arrive(there, t, FAR_X, part)
            self.pass_on(there, t, HAND_FAR, part, self.to_core)

    def handed(self, t):
        core = 1 - self.c
        pltpu.make_async_copy(self.shards[t], self.mine(t, self.z)(), self.local.at[t]).wait()
        for d in range(LINE):
            for there, z in self.at(d):
                for slot, y, h in (
                    (HAND + z, self.y, self.h if d == 3 else None),
                    (HAND_Y + z, 1 - self.y, self.h),
                    (HAND_X + z, 1 - self.y, 1 - self.h),
                ):
                    part = lambda z=z, y=y, h=h: self.part(t, z, y, core, h)
                    self.arrive(there, t, slot, part)
        for there, z in self.sources(3):
            part = lambda z=z: self.part(t, z, self.y, core, 1 - self.h)
            self.arrive(there, t, HAND_FAR, part)

    def event(self, kind, t, d):
        if kind == OWN:
            self.own(t)
        elif kind == OTHER:
            self.other(t)
        else:
            {COME: self.come, TURN: self.turn, LAST: self.last}[kind](t, d)

    def drain(self):
        for condition, make in self.started:
            under(condition, lambda make=make: make().wait_send())


def meet(neighbours):
    barrier = pltpu.get_barrier_semaphore()
    for to in neighbours:
        pl.semaphore_signal(barrier, inc=1, device_id=to, device_id_type=MESH)
    pl.semaphore_wait(barrier, len(neighbours))


def passed_along(shard, axis, by):
    length = lax.axis_size(axis)
    return lax.ppermute(shard, axis, [(i, (i + by) % length) for i in range(length)])


def norm_rows(values_in):
    centre = values_in - jnp.mean(values_in, axis=-1, keepdims=True)
    spread = jnp.mean(centre * centre, axis=-1, keepdims=True)
    return centre * lax.rsqrt(spread + 1e-06)


def restore_grid(region, arrived, offsets, columns):
    widened = jnp.concatenate([region, arrived], axis=2)
    return jax.vmap(lambda plane, shift_by: lax.dynamic_slice_in_dim(plane, shift_by, columns, 1))(
        widened, offsets
    )


def plain(latents, offsets, levels, mod_table, rel_bias, w_qkv, w_out, w_up, w_down):
    batches, lat_rows, columns, features = latents.shape
    inner = HEADS * HEAD_DIM
    per_dev = columns // WIN
    selector = (levels[:, None] == jnp.arange(LEVELS, dtype=jnp.int32)[None, :]).astype(
        jnp.bfloat16
    )
    modulation = jnp.dot(
        selector, mod_table.reshape(LEVELS, 6 * features), preferred_element_type=jnp.float32
    )
    modulation = modulation.reshape(batches, 6, 1, 1, features)
    stream = latents.astype(jnp.float32)
    normed = (norm_rows(stream) * (1.0 + modulation[:, 0]) + modulation[:, 1]).astype(jnp.bfloat16)
    arrived = passed_along(normed[:, :, columns - WIN :, :], "win", 1)
    widened = jnp.concatenate([arrived, normed], axis=2)
    rolled = jax.vmap(
        lambda plane, shift_by: lax.dynamic_slice_in_dim(plane, WIN - shift_by, columns, 1)
    )(widened, offsets)
    full_qkv = lax.all_gather(w_qkv, "win", axis=0, tiled=True)
    windows = rolled.reshape(batches, lat_rows, per_dev, WIN, features).transpose(0, 2, 1, 3, 4)
    windows = windows.reshape(-1, lat_rows * WIN, features)
    number = windows.shape[0]
    triple = jnp.dot(windows.reshape(-1, features), full_qkv, preferred_element_type=jnp.float32)
    triple = triple.astype(jnp.bfloat16).reshape(number, lat_rows * WIN, 3, HEADS, HEAD_DIM)
    scores = jnp.einsum(
        "wqhe,wkhe->whqk", triple[:, :, 0], triple[:, :, 1], preferred_element_type=jnp.float32
    )
    scores = scores * (1.0 / HEAD_DIM**0.5) + rel_bias[None]
    probs = jax.nn.softmax(scores, axis=-1).astype(jnp.bfloat16)
    attended = jnp.einsum(
        "whqk,wkhe->wqhe", probs, triple[:, :, 2], preferred_element_type=jnp.float32
    ).astype(jnp.bfloat16)
    attended = attended.reshape(batches, per_dev, lat_rows, WIN, inner).transpose(0, 2, 1, 3, 4)
    attended = attended.reshape(batches, lat_rows, columns, inner)
    full_out = lax.all_gather(w_out, "win", axis=0, tiled=True)
    returned = passed_along(attended[:, :, :WIN, :], "win", -1)
    restored = restore_grid(attended, returned, offsets, columns)
    projected = jnp.dot(restored.reshape(-1, inner), full_out, preferred_element_type=jnp.float32)
    projected = projected.reshape(batches, lat_rows, columns, features)
    middle = (stream + modulation[:, 2] * projected).astype(jnp.bfloat16)
    second = (
        norm_rows(middle.astype(jnp.float32)) * (1.0 + modulation[:, 3]) + modulation[:, 4]
    ).astype(jnp.bfloat16)
    full_up = lax.all_gather(w_up, "win", axis=0, tiled=True)
    hidden = jnp.dot(second.reshape(-1, features), full_up, preferred_element_type=jnp.float32)
    hidden = jax.nn.gelu(hidden, approximate=False).astype(jnp.bfloat16)
    full_down = lax.all_gather(w_down, "win", axis=0, tiled=True)
    lowered = jnp.dot(hidden, full_down, preferred_element_type=jnp.float32).reshape(
        batches, lat_rows, columns, features
    )
    return (middle.astype(jnp.float32) + modulation[:, 5] * lowered).astype(jnp.bfloat16)


def spread(work, events):
    done = 0
    for index, piece in enumerate(work):
        piece()
        upto = (len(events) * (index + 1)) // len(work)
        for event in events[done:upto]:
            event()
        done = upto


def pieces(count, step, act):
    def piece(first):
        lax.fori_loop(first, min(first + step, count), lambda i, _: (act(i), 0)[1], 0)

    return [functools.partial(piece, first) for first in range(0, count, step)]


def kernel(
    batches, block, area, lat_ref, low_ref, high_ref, mod_ref, gather_in_ref, gather_out_ref,
    bias_ref, s0, s1, s2, s3, out_ref, f0, f1, f2, f3, prev, after, normed, wins, triple, heads,
    restored, middle, second, hidden, send, recv, local, halo_send, halo_recv,
):
    features = lat_ref.shape[1]
    inner = HEADS * HEAD_DIM
    own = lat_ref.shape[0] // batches
    side = low_ref.shape[0] // batches
    wide = own + 2 * side
    moved = wins.shape[0] // batches
    gather = Gather((s0, s1, s2, s3), (f0, f1, f2, f3), send, recv, local)
    me, count = lax.axis_index("win"), lax.axis_size("win")
    right, left = {"win": lax.rem(me + 1, count)}, {"win": lax.rem(me + count - 1, count)}
    meet(gather.neighbours() + [right, left])
    halos = []
    for at, src, dst, to in ((0, high_ref, prev, right), (1, low_ref, after, left)):
        made = pltpu.make_async_remote_copy(
            src_ref=src,
            dst_ref=dst,
            send_sem=halo_send.at[at],
            recv_sem=halo_recv.at[at],
            device_id=to,
            device_id_type=MESH,
        )
        made.start()
        halos.append(made)
    gather.own(0)
    gather.own(1)

    def norm_into(src, first, dst, start, m, scale, shift):
        rows = src[pl.ds(first, block), :].astype(jnp.float32)
        value = norm_rows(rows) * (1.0 + mod_ref[m, pl.ds(scale, 1), :])
        value = value + mod_ref[m, pl.ds(shift, 1), :]
        dst[pl.ds(start, block), :] = value.astype(jnp.bfloat16)

    def norm_own(i):
        for m in range(batches):
            norm_into(lat_ref, m * own + i * block, normed, m * wide + side + i * block, m, 0, 1)

    def norm_side(i):
        if i == 0:
            for made in halos:
                made.wait()
        for m in range(batches):
            for src, base in ((prev, 0), (after, side + own)):
                norm_into(src, m * side + i * block, normed, m * wide + base + i * block, m, 0, 1)

    def arrange(m):
        rows = normed[pl.ds(pl.multiple_of(m * wide, 16), wide), :]
        wins[pl.ds(pl.multiple_of(m * moved, 16), moved), :] = jnp.dot(
            gather_in_ref[m], rows, preferred_element_type=jnp.float32
        ).astype(jnp.bfloat16)

    width = 256

    def columns(i):
        return pl.ds(pl.multiple_of(i * width, width), width)

    def project(i):
        triple[:, columns(i)] = jnp.dot(
            wins[...], f0[:, columns(i)], preferred_element_type=jnp.float32
        ).astype(jnp.bfloat16)

    def attend(w):
        rows = pl.ds(pl.multiple_of(w * area, area), area)
        for head in range(HEADS):
            def of(which):
                return triple[rows, pl.ds(which * inner + head * HEAD_DIM, HEAD_DIM)]

            scores = lax.dot_general(
                of(0), of(1), (((1,), (1,)), ((), ())), preferred_element_type=jnp.float32
            )
            scores = scores * (1.0 / HEAD_DIM**0.5) + bias_ref[head]
            powers = jnp.exp(scores - jnp.max(scores, axis=-1, keepdims=True))
            probs = (powers / jnp.sum(powers, axis=-1, keepdims=True)).astype(jnp.bfloat16)
            heads[rows, pl.ds(head * HEAD_DIM, HEAD_DIM)] = jnp.dot(
                probs, of(2), preferred_element_type=jnp.float32
            ).astype(jnp.bfloat16)

    def restore(m):
        rows = heads[pl.ds(pl.multiple_of(m * moved, 16), moved), :]
        restored[pl.ds(pl.multiple_of(m * own, 16), own), :] = jnp.dot(
            gather_out_ref[m], rows, preferred_element_type=jnp.float32
        ).astype(jnp.bfloat16)

    def add(base_ref, dst, found, which, i):
        for m in range(batches):
            rows = pl.ds(m * own, own)
            change = mod_ref[m, pl.ds(which, 1), columns(i)] * found[m * own : (m + 1) * own]
            dst[rows, columns(i)] = (
                base_ref[rows, columns(i)].astype(jnp.float32) + change
            ).astype(jnp.bfloat16)

    def settle(i):
        found = jnp.dot(restored[...], f1[:, columns(i)], preferred_element_type=jnp.float32)
        add(lat_ref, middle, found, 2, i)

    def lift(i):
        found = jnp.dot(second[...], f2[:, columns(i)], preferred_element_type=jnp.float32)
        found = 0.5 * found * (1.0 + lax.erf(found * (0.5**0.5)))
        hidden[:, columns(i)] = found.astype(jnp.bfloat16)

    def lower(i):
        found = jnp.dot(hidden[...], f3[:, columns(i)], preferred_element_type=jnp.float32)
        add(middle, out_ref, found, 5, i)

    def norm_again(i):
        for m in range(batches):
            at = m * own + i * block
            norm_into(middle, at, second, at, m, 3, 4)

    events = [(t, functools.partial(gather.event, kind, t, d)) for kind, t, d in ORDER]

    def until(*ts):
        index = max([i for i, (t, _) in enumerate(events) if t in ts], default=-1) + 1
        taken = [event for _, event in events[:index]]
        del events[:index]
        return taken

    def each(act, count):
        return [functools.partial(act, i) for i in range(count)]

    def restore_all():
        for m in range(batches):
            restore(m)
        gather.handed(1)

    first = each(norm_own, own // block) + each(norm_side, side // block) + each(arrange, batches)
    early = until(0)
    spread(first, early[: len(first) + 3])
    for event in early[len(first) + 3 :]:
        event()
    gather.handed(0)
    work = pieces(triple.shape[1] // width, 3, project) + pieces(wins.shape[0] // area, 2, attend)
    work += [restore_all] + pieces(features // width, 3, settle) + pieces(own // block, 2, norm_again)
    spread(work, until(2))
    gather.handed(2)
    spread(pieces(hidden.shape[1] // width, 2, lift), until(3))
    gather.handed(3)
    spread(pieces(features // width, features // width, lower), [])
    gather.drain()


def local(latents, offsets, levels, mod_table, rel_bias, w_qkv, w_out, w_up, w_down):
    count = lax.axis_size("win")
    batches, lat_rows, columns, features = latents.shape
    if count != 4 * LINE or lax.axis_size("groups") % 2 or columns < WIN:
        return plain(
            latents, offsets, levels, mod_table, rel_bias, w_qkv, w_out, w_up, w_down
        )
    selector = (levels[:, None] == jnp.arange(LEVELS, dtype=jnp.int32)[None, :]).astype(
        jnp.bfloat16
    )
    modulation = jnp.dot(
        selector, mod_table.reshape(LEVELS, 6 * features), preferred_element_type=jnp.float32
    ).reshape(batches, 6, features)
    area = lat_rows * WIN
    bands = columns // WIN + 1
    own, moved = lat_rows * columns, bands * area
    row = jnp.arange(lat_rows, dtype=jnp.int32)

    def spots(first, size):
        place = first + jnp.arange(size, dtype=jnp.int32)
        both = jnp.broadcast_to(row[:, None], (lat_rows, size)), jnp.broadcast_to(
            place[None], (lat_rows, size)
        )
        return [part.reshape(-1) for part in both]

    def joined(parts):
        return [jnp.concatenate(side) for side in zip(*parts)]

    wide_row, wide_at = joined(
        [spots(0, WIN), spots(WIN, columns), spots(WIN + columns, WIN)]
    )
    rolled_row, rolled_at = joined([spots(band * WIN, WIN) for band in range(bands)])
    own_row, own_at = spots(0, columns)
    by = offsets[:, None, None]
    gather_in = (rolled_row[:, None] == wide_row[None]) & (
        rolled_at[None, :, None] + WIN - by == wide_at[None, None]
    )
    gather_out = (own_row[:, None] == rolled_row[None]) & (
        own_at[None, :, None] + by == rolled_at[None, None]
    )
    low = latents[:, :, :WIN].reshape(-1, features)
    high = latents[:, :, columns - WIN :].reshape(-1, features)
    shards = (w_qkv, w_out, w_up, w_down)
    vmem = pl.BlockSpec(memory_space=pltpu.VMEM)
    total = batches * own
    bf = jnp.bfloat16
    found = pl.pallas_call(
        functools.partial(kernel, batches, 32, area),
        out_shape=jax.ShapeDtypeStruct((total, features), bf),
        in_specs=[vmem] * 11,
        out_specs=vmem,
        scratch_shapes=[pltpu.VMEM((s.shape[0] * count, s.shape[1]), bf) for s in shards]
        + [
            pltpu.VMEM(low.shape, bf),
            pltpu.VMEM(low.shape, bf),
            pltpu.VMEM((batches * (own + 2 * area), features), bf),
            pltpu.VMEM((batches * moved, features), bf),
            pltpu.VMEM((batches * moved, w_qkv.shape[1]), bf),
            pltpu.VMEM((batches * moved, w_out.shape[0] * count), bf),
            pltpu.VMEM((total, w_out.shape[0] * count), bf),
            pltpu.VMEM((total, features), bf),
            pltpu.VMEM((total, features), bf),
            pltpu.VMEM((total, w_up.shape[1]), bf),
            pltpu.SemaphoreType.DMA((4 * SLOTS,)),
            pltpu.SemaphoreType.DMA((4 * SLOTS,)),
            pltpu.SemaphoreType.DMA((4,)),
            pltpu.SemaphoreType.DMA((2,)),
            pltpu.SemaphoreType.DMA((2,)),
        ],
        compiler_params=pltpu.CompilerParams(
            collective_id=0, has_side_effects=True, vmem_limit_bytes=62 * 2**20
        ),
    )(
        latents.reshape(total, features), low, high, modulation, gather_in.astype(bf),
        gather_out.astype(bf), rel_bias, *shards,
    )
    return found.reshape(latents.shape)


def solution(mesh):
    in_specs = (
        P("groups", None, "win", None),
        P("groups"),
        P("groups"),
        P(),
        P(),
        P("win", None),
        P("win", None),
        P("win", None),
        P("win", None),
    )
    out_specs = P("groups", None, "win", None)
    return jax.shard_map(local, mesh=mesh, in_specs=in_specs, out_specs=out_specs, check_vma=False)
```

```python
import functools

import jax
import jax.numpy as jnp
from jax import lax
from jax.experimental import pallas as pl
from jax.experimental.pallas import tpu as pltpu
from jax.sharding import PartitionSpec as P

HEADS = 6
HEAD_DIM = 128
WIN = 8
LEVELS = 32

MESH = pl.DeviceIdType.MESH
SLOTS = 28
LINE = 4
UP, DOWN, ALONG_Y, ALONG_X, FAR_X, HAND, HAND_FAR, HAND_Y, HAND_X = 0, 3, 6, 10, 14, 15, 19, 20, 24

OWN, COME, TURN, LAST, OTHER = range(5)
ORDER = (
    (TURN, 0, 0), (TURN, 1, 0), (COME, 0, 1), (COME, 1, 1), (TURN, 0, 1), (COME, 0, 2),
    (COME, 1, 2), (TURN, 1, 1), (OWN, 2, 0), (LAST, 0, 0), (TURN, 0, 2), (COME, 1, 3),
    (COME, 0, 3), (TURN, 1, 2), (TURN, 1, 3), (LAST, 1, 3), (COME, 2, 1), (TURN, 0, 3),
    (LAST, 1, 0), (TURN, 2, 0), (OTHER, 1, 0), (TURN, 2, 1), (LAST, 1, 2), (OWN, 3, 0),
    (TURN, 3, 0), (OTHER, 0, 0), (LAST, 1, 1), (COME, 2, 2), (LAST, 0, 3), (LAST, 0, 1),
    (LAST, 0, 2), (LAST, 2, 0), (COME, 3, 1), (TURN, 2, 2), (COME, 2, 3), (TURN, 3, 1),
    (COME, 3, 2), (OTHER, 2, 0), (TURN, 2, 3), (LAST, 2, 1), (COME, 3, 3), (LAST, 2, 3),
    (LAST, 2, 2), (TURN, 3, 2), (LAST, 3, 1), (LAST, 3, 0), (TURN, 3, 3), (LAST, 3, 2),
    (OTHER, 3, 0), (LAST, 3, 3),
)


def under(condition, act):
    if condition is None:
        act()
    else:
        pl.when(condition)(act)


class Gather:
    def __init__(self, shards, fulls, send, recv, local):
        self.shards, self.fulls = shards, fulls
        self.send, self.recv, self.local = send, recv, local
        me = lax.axis_index("win")
        self.c = lax.rem(me, 2)
        self.y = lax.rem(me // 2, 2)
        self.z = me // 4
        self.g = lax.axis_index("groups")
        self.h = lax.rem(self.g, 2)
        up, down = lax.rem(self.z + 1, LINE), lax.rem(self.z + LINE - 1, LINE)
        self.to_up = {"win": self.place(up, self.y, self.c)}
        self.to_down = {"win": self.place(down, self.y, self.c)}
        self.to_y = {"win": self.place(self.z, 1 - self.y, self.c)}
        self.to_core = {"win": self.place(self.z, self.y, 1 - self.c)}
        self.to_x = {"groups": self.g + 1 - 2 * self.h}
        self.started = []

    def place(self, z, y, c):
        return (z * 2 + y) * 2 + c

    def neighbours(self):
        return [self.to_up, self.to_down, self.to_y, self.to_core, self.to_x]

    def half(self, t, h):
        width = self.shards[t].shape[1] // 2
        return pl.ds(pl.multiple_of(h * width, 128), width)

    def part(self, t, z, y, c, h=None):
        depth = self.shards[t].shape[0]
        rows = pl.ds(pl.multiple_of(self.place(z, y, c) * depth, depth), depth)
        return self.fulls[t].at[rows] if h is None else self.fulls[t].at[rows, self.half(t, h)]

    def copy(self, t, slot, src, dst, to):
        at = t * SLOTS + slot
        return pltpu.make_async_remote_copy(
            src_ref=src,
            dst_ref=dst,
            send_sem=self.send.at[at],
            recv_sem=self.recv.at[at],
            device_id=to,
            device_id_type=MESH,
        )

    def put(self, condition, make):
        under(condition, lambda: make().start())
        self.started.append((condition, make))

    def pass_on(self, condition, t, slot, part, to):
        self.put(condition, lambda: self.copy(t, slot, part(), part(), to))

    def arrive(self, condition, t, slot, part):
        under(condition, lambda: self.copy(t, slot, part(), part(), self.to_core).wait_recv())

    def mine(self, t, z, h=None):
        return lambda: self.part(t, z, self.y, self.c, h)

    def own(self, t):
        shard = self.shards[t]
        mine, half = self.mine(t, self.z), self.mine(t, self.z, self.h)
        up, down = self.z + 1 < LINE, self.z >= 1
        self.put(up, lambda: self.copy(t, UP, shard, mine(), self.to_up))
        self.put(down, lambda: self.copy(t, DOWN, shard, mine(), self.to_down))
        source = shard.at[:, self.half(t, self.h)]
        self.put(None, lambda: self.copy(t, ALONG_Y + self.z, source, half(), self.to_y))
        self.put(None, lambda: self.copy(t, HAND + self.z, shard, mine(), self.to_core))
        pltpu.make_async_copy(shard, mine(), self.local.at[t]).start()

    def sources(self, d):
        return ((self.z >= d, self.z - d), (self.z + d < LINE, self.z + d))

    def come(self, t, d):
        ways = ((UP, self.z + 1 < LINE, self.to_up), (DOWN, self.z >= 1, self.to_down))
        h = self.h if d == 3 else None
        for (there, z), (way, more, to) in zip(self.sources(d), ways):
            part = self.mine(t, z, h)
            self.arrive(there, t, way + d - 1, part)
            if d < 3:
                onward = self.mine(t, z, self.h if d == 2 else None)
                self.pass_on(there & more, t, way + d, onward, to)
            self.pass_on(there, t, ALONG_Y + z, self.mine(t, z, self.h), self.to_y)
            if d == 3:
                self.pass_on(there, t, FAR_X, part, self.to_x)
            self.pass_on(there, t, HAND + z, part, self.to_core)

    def at(self, d):
        return ((None, self.z),) if d == 0 else self.sources(d)

    def turn(self, t, d):
        for there, z in self.at(d):
            part = lambda z=z: self.part(t, z, 1 - self.y, self.c, self.h)
            self.arrive(there, t, ALONG_Y + z, part)
            self.pass_on(there, t, ALONG_X + z, part, self.to_x)
            self.pass_on(there, t, HAND_Y + z, part, self.to_core)

    def last(self, t, d):
        for there, z in self.at(d):
            part = lambda z=z: self.part(t, z, 1 - self.y, self.c, 1 - self.h)
            self.arrive(there, t, ALONG_X + z, part)
            self.pass_on(there, t, HAND_X + z, part, self.to_core)

    def other(self, t):
        for there, z in self.sources(3):
            part = self.mine(t, z, 1 - self.h)
            self.arrive(there, t, FAR_X, part)
            self.pass_on(there, t, HAND_FAR, part, self.to_core)

    def handed(self, t):
        core = 1 - self.c
        pltpu.make_async_copy(self.shards[t], self.mine(t, self.z)(), self.local.at[t]).wait()
        for d in range(LINE):
            for there, z in self.at(d):
                for slot, y, h in (
                    (HAND + z, self.y, self.h if d == 3 else None),
                    (HAND_Y + z, 1 - self.y, self.h),
                    (HAND_X + z, 1 - self.y, 1 - self.h),
                ):
                    part = lambda z=z, y=y, h=h: self.part(t, z, y, core, h)
                    self.arrive(there, t, slot, part)
        for there, z in self.sources(3):
            part = lambda z=z: self.part(t, z, self.y, core, 1 - self.h)
            self.arrive(there, t, HAND_FAR, part)

    def event(self, kind, t, d):
        if kind == OWN:
            self.own(t)
        elif kind == OTHER:
            self.other(t)
        else:
            {COME: self.come, TURN: self.turn, LAST: self.last}[kind](t, d)

    def drain(self):
        for condition, make in self.started:
            under(condition, lambda make=make: make().wait_send())


def meet(neighbours):
    barrier = pltpu.get_barrier_semaphore()
    for to in neighbours:
        pl.semaphore_signal(barrier, inc=1, device_id=to, device_id_type=MESH)
    pl.semaphore_wait(barrier, len(neighbours))


def passed_along(shard, axis, by):
    length = lax.axis_size(axis)
    return lax.ppermute(shard, axis, [(i, (i + by) % length) for i in range(length)])


def norm_rows(values_in):
    centre = values_in - jnp.mean(values_in, axis=-1, keepdims=True)
    spread = jnp.mean(centre * centre, axis=-1, keepdims=True)
    return centre * lax.rsqrt(spread + 1e-06)


def restore_grid(region, arrived, offsets, columns):
    widened = jnp.concatenate([region, arrived], axis=2)
    return jax.vmap(lambda plane, shift_by: lax.dynamic_slice_in_dim(plane, shift_by, columns, 1))(
        widened, offsets
    )


def plain(latents, offsets, levels, mod_table, rel_bias, w_qkv, w_out, w_up, w_down):
    batches, lat_rows, columns, features = latents.shape
    inner = HEADS * HEAD_DIM
    per_dev = columns // WIN
    selector = (levels[:, None] == jnp.arange(LEVELS, dtype=jnp.int32)[None, :]).astype(
        jnp.bfloat16
    )
    modulation = jnp.dot(
        selector, mod_table.reshape(LEVELS, 6 * features), preferred_element_type=jnp.float32
    )
    modulation = modulation.reshape(batches, 6, 1, 1, features)
    stream = latents.astype(jnp.float32)
    normed = (norm_rows(stream) * (1.0 + modulation[:, 0]) + modulation[:, 1]).astype(jnp.bfloat16)
    arrived = passed_along(normed[:, :, columns - WIN :, :], "win", 1)
    widened = jnp.concatenate([arrived, normed], axis=2)
    rolled = jax.vmap(
        lambda plane, shift_by: lax.dynamic_slice_in_dim(plane, WIN - shift_by, columns, 1)
    )(widened, offsets)
    full_qkv = lax.all_gather(w_qkv, "win", axis=0, tiled=True)
    windows = rolled.reshape(batches, lat_rows, per_dev, WIN, features).transpose(0, 2, 1, 3, 4)
    windows = windows.reshape(-1, lat_rows * WIN, features)
    number = windows.shape[0]
    triple = jnp.dot(windows.reshape(-1, features), full_qkv, preferred_element_type=jnp.float32)
    triple = triple.astype(jnp.bfloat16).reshape(number, lat_rows * WIN, 3, HEADS, HEAD_DIM)
    scores = jnp.einsum(
        "wqhe,wkhe->whqk", triple[:, :, 0], triple[:, :, 1], preferred_element_type=jnp.float32
    )
    scores = scores * (1.0 / HEAD_DIM**0.5) + rel_bias[None]
    probs = jax.nn.softmax(scores, axis=-1).astype(jnp.bfloat16)
    attended = jnp.einsum(
        "whqk,wkhe->wqhe", probs, triple[:, :, 2], preferred_element_type=jnp.float32
    ).astype(jnp.bfloat16)
    attended = attended.reshape(batches, per_dev, lat_rows, WIN, inner).transpose(0, 2, 1, 3, 4)
    attended = attended.reshape(batches, lat_rows, columns, inner)
    full_out = lax.all_gather(w_out, "win", axis=0, tiled=True)
    returned = passed_along(attended[:, :, :WIN, :], "win", -1)
    restored = restore_grid(attended, returned, offsets, columns)
    projected = jnp.dot(restored.reshape(-1, inner), full_out, preferred_element_type=jnp.float32)
    projected = projected.reshape(batches, lat_rows, columns, features)
    middle = (stream + modulation[:, 2] * projected).astype(jnp.bfloat16)
    second = (
        norm_rows(middle.astype(jnp.float32)) * (1.0 + modulation[:, 3]) + modulation[:, 4]
    ).astype(jnp.bfloat16)
    full_up = lax.all_gather(w_up, "win", axis=0, tiled=True)
    hidden = jnp.dot(second.reshape(-1, features), full_up, preferred_element_type=jnp.float32)
    hidden = jax.nn.gelu(hidden, approximate=False).astype(jnp.bfloat16)
    full_down = lax.all_gather(w_down, "win", axis=0, tiled=True)
    lowered = jnp.dot(hidden, full_down, preferred_element_type=jnp.float32).reshape(
        batches, lat_rows, columns, features
    )
    return (middle.astype(jnp.float32) + modulation[:, 5] * lowered).astype(jnp.bfloat16)


def spread(work, events):
    done = 0
    for index, piece in enumerate(work):
        piece()
        upto = (len(events) * (index + 1)) // len(work)
        for event in events[done:upto]:
            event()
        done = upto


def pieces(count, step, act):
    def piece(first):
        lax.fori_loop(first, min(first + step, count), lambda i, _: (act(i), 0)[1], 0)

    return [functools.partial(piece, first) for first in range(0, count, step)]


def kernel(
    batches, block, area, lat_ref, low_ref, high_ref, mod_ref, gather_in_ref, gather_out_ref,
    bias_ref, s0, s1, s2, s3, out_ref, f0, f1, f2, f3, prev, after, normed, wins, triple, heads,
    restored, middle, second, hidden, send, recv, local, halo_send, halo_recv,
):
    features = lat_ref.shape[1]
    inner = HEADS * HEAD_DIM
    own = lat_ref.shape[0] // batches
    side = low_ref.shape[0] // batches
    wide = own + 2 * side
    moved = wins.shape[0] // batches
    gather = Gather((s0, s1, s2, s3), (f0, f1, f2, f3), send, recv, local)
    me, count = lax.axis_index("win"), lax.axis_size("win")
    right, left = {"win": lax.rem(me + 1, count)}, {"win": lax.rem(me + count - 1, count)}
    meet(gather.neighbours() + [right, left])
    gather.own(0)
    halos = []
    for at, src, dst, to in ((0, high_ref, prev, right), (1, low_ref, after, left)):
        made = pltpu.make_async_remote_copy(
            src_ref=src,
            dst_ref=dst,
            send_sem=halo_send.at[at],
            recv_sem=halo_recv.at[at],
            device_id=to,
            device_id_type=MESH,
        )
        made.start()
        halos.append(made)
    gather.own(1)

    def norm_into(src, first, dst, start, m, scale, shift):
        rows = src[pl.ds(first, block), :].astype(jnp.float32)
        value = norm_rows(rows) * (1.0 + mod_ref[m, pl.ds(scale, 1), :])
        value = value + mod_ref[m, pl.ds(shift, 1), :]
        dst[pl.ds(start, block), :] = value.astype(jnp.bfloat16)

    def norm_own(i):
        for m in range(batches):
            norm_into(lat_ref, m * own + i * block, normed, m * wide + side + i * block, m, 0, 1)

    def norm_side(i):
        if i == 0:
            for made in halos:
                made.wait()
        for m in range(batches):
            for src, base in ((prev, 0), (after, side + own)):
                norm_into(src, m * side + i * block, normed, m * wide + base + i * block, m, 0, 1)

    def arrange(m):
        rows = normed[pl.ds(pl.multiple_of(m * wide, 16), wide), :]
        wins[pl.ds(pl.multiple_of(m * moved, 16), moved), :] = jnp.dot(
            gather_in_ref[m], rows, preferred_element_type=jnp.float32
        ).astype(jnp.bfloat16)

    width = 256

    def columns(i):
        return pl.ds(pl.multiple_of(i * width, width), width)

    def project(i):
        triple[:, columns(i)] = jnp.dot(
            wins[...], f0[:, columns(i)], preferred_element_type=jnp.float32
        ).astype(jnp.bfloat16)

    def attend(w):
        rows = pl.ds(pl.multiple_of(w * area, area), area)
        for head in range(HEADS):
            def of(which):
                return triple[rows, pl.ds(which * inner + head * HEAD_DIM, HEAD_DIM)]

            scores = lax.dot_general(
                of(0), of(1), (((1,), (1,)), ((), ())), preferred_element_type=jnp.float32
            )
            scores = scores * (1.0 / HEAD_DIM**0.5) + bias_ref[head]
            powers = jnp.exp(scores - jnp.max(scores, axis=-1, keepdims=True))
            probs = (powers / jnp.sum(powers, axis=-1, keepdims=True)).astype(jnp.bfloat16)
            heads[rows, pl.ds(head * HEAD_DIM, HEAD_DIM)] = jnp.dot(
                probs, of(2), preferred_element_type=jnp.float32
            ).astype(jnp.bfloat16)

    def restore(m):
        rows = heads[pl.ds(pl.multiple_of(m * moved, 16), moved), :]
        restored[pl.ds(pl.multiple_of(m * own, 16), own), :] = jnp.dot(
            gather_out_ref[m], rows, preferred_element_type=jnp.float32
        ).astype(jnp.bfloat16)

    def add(base_ref, dst, found, which, i):
        for m in range(batches):
            rows = pl.ds(m * own, own)
            change = mod_ref[m, pl.ds(which, 1), columns(i)] * found[m * own : (m + 1) * own]
            dst[rows, columns(i)] = (
                base_ref[rows, columns(i)].astype(jnp.float32) + change
            ).astype(jnp.bfloat16)

    def settle(i):
        found = jnp.dot(restored[...], f1[:, columns(i)], preferred_element_type=jnp.float32)
        add(lat_ref, middle, found, 2, i)

    def lift(i):
        found = jnp.dot(second[...], f2[:, columns(i)], preferred_element_type=jnp.float32)
        found = 0.5 * found * (1.0 + lax.erf(found * (0.5**0.5)))
        hidden[:, columns(i)] = found.astype(jnp.bfloat16)

    def lower(i):
        found = jnp.dot(hidden[...], f3[:, columns(i)], preferred_element_type=jnp.float32)
        add(middle, out_ref, found, 5, i)

    def norm_again(i):
        for m in range(batches):
            at = m * own + i * block
            norm_into(middle, at, second, at, m, 3, 4)

    events = [(t, functools.partial(gather.event, kind, t, d)) for kind, t, d in ORDER]

    def until(*ts):
        index = max([i for i, (t, _) in enumerate(events) if t in ts], default=-1) + 1
        taken = [event for _, event in events[:index]]
        del events[:index]
        return taken

    def each(act, count):
        return [functools.partial(act, i) for i in range(count)]

    def restore_all():
        for m in range(batches):
            restore(m)
        gather.handed(1)

    first = each(norm_own, own // block) + each(norm_side, side // block) + each(arrange, batches)
    early = until(0)
    spread(first, early[: len(first) + 3])
    for event in early[len(first) + 3 :]:
        event()
    gather.handed(0)
    work = pieces(triple.shape[1] // width, 3, project) + pieces(wins.shape[0] // area, 2, attend)
    work += [restore_all] + pieces(features // width, 3, settle) + pieces(own // block, 2, norm_again)
    spread(work, until(2))
    gather.handed(2)
    spread(pieces(hidden.shape[1] // width, 2, lift), until(3))
    gather.handed(3)
    spread(pieces(features // width, features // width, lower), [])
    gather.drain()


def local(latents, offsets, levels, mod_table, rel_bias, w_qkv, w_out, w_up, w_down):
    count = lax.axis_size("win")
    batches, lat_rows, columns, features = latents.shape
    if count != 4 * LINE or lax.axis_size("groups") % 2 or columns < WIN:
        return plain(
            latents, offsets, levels, mod_table, rel_bias, w_qkv, w_out, w_up, w_down
        )
    selector = (levels[:, None] == jnp.arange(LEVELS, dtype=jnp.int32)[None, :]).astype(
        jnp.bfloat16
    )
    modulation = jnp.dot(
        selector, mod_table.reshape(LEVELS, 6 * features), preferred_element_type=jnp.float32
    ).reshape(batches, 6, features)
    area = lat_rows * WIN
    bands = columns // WIN + 1
    own, moved = lat_rows * columns, bands * area
    row = jnp.arange(lat_rows, dtype=jnp.int32)

    def spots(first, size):
        place = first + jnp.arange(size, dtype=jnp.int32)
        both = jnp.broadcast_to(row[:, None], (lat_rows, size)), jnp.broadcast_to(
            place[None], (lat_rows, size)
        )
        return [part.reshape(-1) for part in both]

    def joined(parts):
        return [jnp.concatenate(side) for side in zip(*parts)]

    wide_row, wide_at = joined(
        [spots(0, WIN), spots(WIN, columns), spots(WIN + columns, WIN)]
    )
    rolled_row, rolled_at = joined([spots(band * WIN, WIN) for band in range(bands)])
    own_row, own_at = spots(0, columns)
    by = offsets[:, None, None]
    gather_in = (rolled_row[:, None] == wide_row[None]) & (
        rolled_at[None, :, None] + WIN - by == wide_at[None, None]
    )
    gather_out = (own_row[:, None] == rolled_row[None]) & (
        own_at[None, :, None] + by == rolled_at[None, None]
    )
    low = latents[:, :, :WIN].reshape(-1, features)
    high = latents[:, :, columns - WIN :].reshape(-1, features)
    shards = (w_qkv, w_out, w_up, w_down)
    vmem = pl.BlockSpec(memory_space=pltpu.VMEM)
    total = batches * own
    bf = jnp.bfloat16
    found = pl.pallas_call(
        functools.partial(kernel, batches, 32, area),
        out_shape=jax.ShapeDtypeStruct((total, features), bf),
        in_specs=[vmem] * 11,
        out_specs=vmem,
        scratch_shapes=[pltpu.VMEM((s.shape[0] * count, s.shape[1]), bf) for s in shards]
        + [
            pltpu.VMEM(low.shape, bf),
            pltpu.VMEM(low.shape, bf),
            pltpu.VMEM((batches * (own + 2 * area), features), bf),
            pltpu.VMEM((batches * moved, features), bf),
            pltpu.VMEM((batches * moved, w_qkv.shape[1]), bf),
            pltpu.VMEM((batches * moved, w_out.shape[0] * count), bf),
            pltpu.VMEM((total, w_out.shape[0] * count), bf),
            pltpu.VMEM((total, features), bf),
            pltpu.VMEM((total, features), bf),
            pltpu.VMEM((total, w_up.shape[1]), bf),
            pltpu.SemaphoreType.DMA((4 * SLOTS,)),
            pltpu.SemaphoreType.DMA((4 * SLOTS,)),
            pltpu.SemaphoreType.DMA((4,)),
            pltpu.SemaphoreType.DMA((2,)),
            pltpu.SemaphoreType.DMA((2,)),
        ],
        compiler_params=pltpu.CompilerParams(
            collective_id=0, has_side_effects=True, vmem_limit_bytes=62 * 2**20
        ),
    )(
        latents.reshape(total, features), low, high, modulation, gather_in.astype(bf),
        gather_out.astype(bf), rel_bias, *shards,
    )
    return found.reshape(latents.shape)


def solution(mesh):
    in_specs = (
        P("groups", None, "win", None),
        P("groups"),
        P("groups"),
        P(),
        P(),
        P("win", None),
        P("win", None),
        P("win", None),
        P("win", None),
    )
    out_specs = P("groups", None, "win", None)
    return jax.shard_map(local, mesh=mesh, in_specs=in_specs, out_specs=out_specs, check_vma=False)
```
